512 devices in a mesh: tm: 128 (over z, y, core), col: 4 (over x).
Axes of the slice: x: 4, y: 4, z: 16, core: 2. Of those that a mesh axis runs over, the one named last changes fastest.
Arguments:
- gain: float32 [128, 256, 256], P('tm', None, 'col')
- offset: float32 [128, 256], P('tm'), may hold values from -4 to 4
- sub_offset: float32 [128, 8, 256], P('tm'), may hold values from -6 to 6
- terminal_state: float32 [256], replicated, may hold values from -6 to 6
- terminal_factor: float32 [256, 256], replicated, may hold values from -0.375 to 0.375
- obs_rows: bfloat16 [131072, 256], P('tm', 'col'), may hold values from -0.375 to 0.375
- obs_count: int32 [128], P('tm'), may hold values from 256 to 1024, as said below
- obs_step: int32 [131072], P('tm'), may hold values from 0 to 7
Outputs:
- predicted: float32 [131072], P('tm')
- leverage: float32 [131072], P('tm')
The draws below stay inside these ranges and needn't reach their ends.
Inputs may be any that keep to these rules, and one draw needn't show every extreme that they name: `obs_count`: each group has at least a quarter of its slots live; some group has all 1024 live.
All inputs are finite; a program needn't handle non-finite values.
Results may differ from the reference program's by a relative error of at most 0.0029.
Values may be sent and summed in bfloat16 or wider, within the bound.
No kernel may reach another device: no remote copies, remote signals or barrier semaphores. Data moves between devices by JAX's collectives and lax.ppermute only.
A program may use at most 64 MiB of HBM per device.

```python
import jax
import jax.numpy as jnp
from jax import lax

S = 256
SUB = 8
OBS_DEV = 1024
GROUPS = 128
OBS = 131072


def draw_gain(key, part):
    first = jax.random.fold_in(key, 11)
    second = jax.random.fold_in(key, 12)
    spread = jax.random.normal(first, (GROUPS, S, S), jnp.float32) * (0.2 / S ** 0.5)
    diagonal = jax.random.uniform(second, (GROUPS, S), jnp.float32, 0.96, 1.0)
    return spread + diagonal[:, :, None] * jnp.eye(S, dtype=jnp.float32)[None, :, :]


def draw_obs_count(key, part):
    first = jax.random.fold_in(key, 21)
    second = jax.random.fold_in(key, 22)
    counts = jax.random.randint(first, (GROUPS,), OBS_DEV // 4, OBS_DEV + 1)
    where = jax.random.randint(second, (), 0, GROUPS)
    return counts.at[where].set(OBS_DEV).astype(jnp.int32)


def plant(entries, stream_key, least, top_value):
    extent = entries.shape
    index_at = [jax.random.randint(jax.random.fold_in(stream_key, axis), (), 0, extent[axis]) for axis in range(len(extent))]
    entries = entries.at[tuple(index_at)].set(least)
    longest = extent.index(max(extent))
    index_at[longest] = (index_at[longest] + 1) % extent[longest]
    return entries.at[tuple(index_at)].set(top_value)


def block_levels(key, dims, cuts, smallest, largest):
    level = 1.0
    for dim, blocks in cuts:
        steps = jax.random.uniform(jax.random.fold_in(jax.random.fold_in(key, 6), dim), (blocks,), jnp.float32, smallest / len(cuts), largest / len(cuts))
        level = level * jnp.repeat(jnp.exp(steps), dims[dim] // blocks).reshape((-1,) + (1,) * (len(dims) - 1 - dim))
    return level


def centred(own_key, extent, width, limit, shards=(), kind=jnp.bfloat16):
    drawn = jax.random.normal(own_key, extent, jnp.float32) * width
    if len(shards) > 0:
        drawn = block_levels(own_key, extent, shards, -0.22, 0.18) * drawn
    return jnp.clip(drawn, min=-limit, max=limit).astype(kind)


def setup_inputs(seed: int = 0) -> dict:
    splits = jax.random.split(jax.random.key(seed), 9)
    return {
        "gain": draw_gain(jax.random.fold_in(splits[8], 71), 0),
        "offset": centred(splits[1], (GROUPS, S), 0.3, 4.0, ((0, 128),), jnp.float32),
        "sub_offset": centred(splits[2], (GROUPS, SUB, S), 1.0, 6.0, ((0, 128),), jnp.float32),
        "terminal_state": centred(splits[3], (S,), 1.0, 6.0, (), jnp.float32),
        "terminal_factor": centred(splits[4], (S, S), S ** -0.5, 0.375, (), jnp.float32),
        "obs_rows": centred(splits[5], (OBS, S), S ** -0.5, 0.375, ((0, 128), (1, 4))),
        "obs_count": draw_obs_count(jax.random.fold_in(splits[8], 71), 0),
        "obs_step": plant(jax.random.randint(splits[7], (OBS,), 0, SUB), jax.random.fold_in(splits[7], 1), 0, SUB - 1).astype(jnp.int32),
    }


def reference(gain, offset, sub_offset, terminal_state, terminal_factor, obs_rows, obs_count, obs_step):
    highest = lax.Precision.HIGHEST
    rows_all = obs_rows.reshape(GROUPS, OBS_DEV, S)
    steps_all = obs_step.reshape(GROUPS, OBS_DEV)
    slot_ids = jnp.arange(OBS_DEV).astype(jnp.int32)
    step_ids = jnp.arange(SUB).astype(jnp.int32)

    def one_group(carry, item):
        composed, shifted = carry
        block, bias, subs, rows, count, steps = item
        upcoming = jnp.dot(composed, terminal_state, precision=highest) + shifted
        state = jnp.dot(block, upcoming, precision=highest) + bias
        full_map = jnp.dot(block, composed, precision=highest)
        factor = jnp.dot(full_map, terminal_factor, precision=highest,
                         preferred_element_type=jnp.float32).astype(jnp.bfloat16)
        states = (state[None, :] + subs).astype(jnp.bfloat16)
        picks = jnp.dot(rows, states.T, preferred_element_type=jnp.float32)
        onehot = steps[:, None] == step_ids[None, :]
        guess = jnp.sum(jnp.where(onehot, picks, jnp.float32(0.0)), axis=1)
        projected = jnp.dot(rows, factor, preferred_element_type=jnp.float32)
        spread = jnp.sum(projected * projected, axis=1)
        live = (slot_ids < count).astype(jnp.float32)
        new_shift = jnp.dot(block, shifted, precision=highest) + bias
        return (full_map, new_shift), (guess * live, spread * live)

    start = (jnp.eye(S, dtype=jnp.float32), jnp.zeros((S,), jnp.float32))
    items = (gain, offset, sub_offset, rows_all, obs_count, steps_all)
    unused, outs = lax.scan(one_group, start, items, reverse=True)
    return outs[0].reshape(OBS), outs[1].reshape(OBS)
```

```python
import jax
import jax.numpy as jnp
from jax import lax
from jax.sharding import Mesh, PartitionSpec as P

S = 256
SUB = 8
AUG = 264
NZ, NY, NC, NX = 16, 4, 2, 4
TM = ("z", "y", "core")
HIGHEST = lax.Precision.HIGHEST


def tm_id(z, y, c):
    return (z * NY + y) * NC + c


def bias_rows(vec, rows):
    return jnp.zeros((rows, S), jnp.float32).at[rows - SUB].set(vec)


def augment(mat_t, vec):
    tail = jnp.zeros((SUB, S), jnp.float32).at[0].set(vec)
    return jnp.concatenate([mat_t, tail], axis=0)


def after(outer, inner):
    bias = jnp.concatenate([jnp.zeros((inner.shape[0] - SUB, S), jnp.float32), outer[S:]], axis=0)
    return jnp.dot(inner, outer[:S], precision=HIGHEST) + bias


def z_pairs(dist, src_planes):
    return [
        (tm_id(z, y, 0), tm_id(z - dist, y, 0)) for z in src_planes for y in range(NY)
    ]


def pack(carry):
    cols = carry[:64]
    state = carry[64:]
    high = lax.reduce_precision(state, 8, 7)
    low = state - high
    return jnp.concatenate([cols, high, low], axis=0).astype(jnp.bfloat16)


def unpack(packed):
    wide = packed.astype(jnp.float32)
    return jnp.concatenate([wide[:64], wide[64:72] + wide[72:80]], axis=0)


def shards(
    gain, offset, sub_offset, terminal_state, terminal_factor, obs_rows, obs_count, obs_step
):
    core = lax.axis_index("core")
    z = lax.axis_index("z")
    y = lax.axis_index("y")
    x = lax.axis_index("col")
    width = S // NX
    eye = augment(jnp.eye(S, dtype=jnp.float32), jnp.zeros((S,), jnp.float32))

    own_t = gain[0].T
    full_t = lax.all_to_all(jnp.broadcast_to(own_t, (NX, width, S)), "col", 0, 0).reshape(S, S)
    own = augment(full_t, offset[0])
    other = lax.ppermute(own, "core", [(0, 1), (1, 0)])
    first = jnp.where(core == 0, own, other)
    second = jnp.where(core == 0, other, own)
    pair = after(first, second)

    pairs = lax.all_to_all(jnp.broadcast_to(pair, (NY, AUG, S)), "y", 0, 0)
    tail2 = after(pairs[2], pairs[3])
    tail3 = after(pairs[1], tail2)
    plane = after(pairs[0], tail3)

    next_plane = lax.ppermute(plane, TM, z_pairs(1, range(1, NZ)))
    next_plane = jnp.where(z < NZ - 1, next_plane, eye)
    two = after(plane, next_plane)
    next_two = lax.ppermute(two, TM, z_pairs(2, range(2, NZ)))
    next_two = jnp.where(z < NZ - 2, next_two, eye)
    four = after(two, next_two)
    three = after(next_plane, next_two)

    term_cols = lax.dynamic_slice_in_dim(terminal_factor, x * width, width, 1).T
    top = augment(term_cols, terminal_state)
    carry = after(four, top)
    reached = top
    for step in range(1, 4):
        lo = NZ - 4 * (step + 1)
        sent = lax.ppermute(pack(carry), TM, z_pairs(4, range(lo + 4, lo + 8)))
        got = unpack(sent)
        here = jnp.logical_and(z >= lo, z < lo + 4)
        reached = jnp.where(here, got, reached)
        if step < 3:
            carry = jnp.where(here, after(four, got), carry)
    entry = pack(after(three, reached))
    crossed = lax.ppermute(entry, "core", [(0, 1)])
    entry = unpack(jnp.where(core == 0, entry, crossed))

    beyond = jnp.where(y == 0, tail3, jnp.where(y == 1, tail2, jnp.where(y == 2, pairs[3], eye)))
    group = after(jnp.where(core == 0, pair, own), beyond)
    final = after(group, entry)
    factor_t = final[:width].astype(jnp.bfloat16)
    states = (final[width][None, :] + sub_offset[0]).astype(jnp.bfloat16)

    rows_t = obs_rows.T
    pieces = [rows_t] + [
        lax.ppermute(rows_t, "col", [(i, (i + s) % NX) for i in range(NX)]) for s in (1, 2, 3)
    ]
    all_rows = jnp.zeros((S, rows_t.shape[1]), jnp.bfloat16)
    for s in range(NX):
        at = lax.rem(x - s + NX, NX) * width
        all_rows = lax.dynamic_update_slice_in_dim(all_rows, pieces[s], at, 0)

    picks = jnp.dot(states, all_rows, preferred_element_type=jnp.float32)
    onehot = obs_step[None, :] == jnp.arange(SUB)[:, None]
    guess = jnp.sum(jnp.where(onehot, picks, jnp.float32(0.0)), axis=0)
    projected = jnp.dot(factor_t, all_rows, preferred_element_type=jnp.float32)
    spread = lax.psum(jnp.sum(projected * projected, axis=0), "col")
    live = (jnp.arange(rows_t.shape[1]) < obs_count[0]).astype(jnp.float32)
    return (guess * live, spread * live)


def solution(mesh):
    torus = Mesh(mesh.devices.reshape(NZ, NY, NC, NX), ("z", "y", "core", "col"))
    in_specs = (
        P(TM, None, "col"),
        P(TM, None),
        P(TM, None, None),
        P(),
        P(),
        P(TM, "col"),
        P(TM),
        P(TM),
    )
    out_specs = (P(TM), P(TM))
    return jax.shard_map(
        shards, mesh=torus, in_specs=in_specs, out_specs=out_specs, check_vma=False
    )
```

```python
import jax
import jax.numpy as jnp
from jax import lax
from jax.sharding import Mesh, PartitionSpec as P

S = 256
SUB = 8
NZ, NY, NC, NX = 16, 4, 2, 4
WIDTH = S // NX
TM = ("z", "y", "core")
FINE = lax.Precision.HIGH


def tm_id(z, y, c):
    return (z * NY + y) * NC + c


def along_z(moves):
    return [(tm_id(a, y, 0), tm_id(b, y, 0)) for a, b in moves for y in range(NY)]


def tail_rows(vec):
    return jnp.zeros((SUB, S), jnp.float32).at[0].set(vec)


def after(outer, inner):
    rows = inner.shape[0] - SUB
    bias = jnp.concatenate([jnp.zeros((rows, S), jnp.float32), outer[S:]], axis=0)
    return jnp.dot(inner, outer[:S], precision=FINE) + bias


def pack(carry):
    state = carry[WIDTH:]
    high = lax.reduce_precision(state, 8, 7)
    low = state - high
    return jnp.concatenate([carry[:WIDTH], high, low], axis=0).astype(jnp.bfloat16)


def unpack(packed):
    wide = packed.astype(jnp.float32)
    state = wide[WIDTH : WIDTH + SUB] + wide[WIDTH + SUB :]
    return jnp.concatenate([wide[:WIDTH], state], axis=0)


def maps_of(raw, y):
    block = raw[y * NX : (y + 1) * NX, :WIDTH].reshape(S, S)
    return jnp.concatenate([block, raw[y * NX, WIDTH:]], axis=0)


def shards(
    gain, offset, sub_offset, terminal_state, terminal_factor, obs_rows, obs_count, obs_step
):
    core = lax.axis_index("core")
    z = lax.axis_index("z")
    y = lax.axis_index("y")
    x = lax.axis_index("col")
    place = lax.rem(z, 4)
    eye = jnp.eye(S + SUB, S, dtype=jnp.float32)

    own = jnp.concatenate([gain[0].T, tail_rows(offset[0])], axis=0)
    own = lax.all_to_all(
        jnp.broadcast_to(own, (NY * NX, WIDTH + SUB, S)), ("y", "col"), 0, 0
    )
    other = lax.ppermute(own, "core", [(0, 1), (1, 0)])
    even = jnp.where(core == 0, own, other)
    odd = jnp.where(core == 0, other, own)
    pairs = [after(maps_of(even, i), maps_of(odd, i)) for i in range(NY)]
    tail2 = after(pairs[2], pairs[3])
    tail3 = after(pairs[1], tail2)
    plane = after(pairs[0], tail3)

    near = lax.ppermute(
        plane, TM, along_z([(b + j + 1, b + j) for b in range(0, NZ, 4) for j in range(3)])
    )
    near = jnp.where(place == 3, eye, near)
    two = after(plane, near)
    far0 = lax.ppermute(two, TM, along_z([(b + 2, b) for b in range(0, NZ, 4)]))
    far1 = lax.ppermute(two, TM, along_z([(b + 3, b + 1) for b in range(0, NZ, 4)]))
    far = jnp.where(place == 0, far0, jnp.where(place == 1, far1, eye))
    whole = after(two, far0)
    inside = after(near, far)

    term_cols = lax.dynamic_slice_in_dim(terminal_factor, x * WIDTH, WIDTH, 1).T
    top = jnp.concatenate([term_cols, tail_rows(terminal_state)], axis=0)
    head12 = pack(after(whole, top))
    at8 = lax.ppermute(head12, TM, along_z([(12, 8)]))
    head8 = pack(after(whole, unpack(at8)))
    at4 = lax.ppermute(head8, TM, along_z([(8, 4)]))
    head4 = pack(after(whole, unpack(at4)))
    head = jnp.where(z == 12, head12, jnp.where(z == 8, head8, head4))
    at0 = lax.ppermute(head, TM, along_z([(4, 0)]))
    fans = [
        lax.ppermute(head, TM, along_z([(b + 4, b + j) for b in (0, 4, 8)])) for j in (1, 2, 3)
    ]
    reached = jnp.where(z == 8, at8, jnp.where(z == 4, at4, at0))
    for j in (1, 2, 3):
        reached = jnp.where(place == j, fans[j - 1], reached)
    reached = jnp.where(z >= 12, top, unpack(reached))
    entry = pack(after(inside, reached))
    crossed = lax.ppermute(entry, "core", [(0, 1)])
    entry = unpack(jnp.where(core == 0, entry, crossed))

    beyond = jnp.where(
        y == 0, tail3, jnp.where(y == 1, tail2, jnp.where(y == 2, pairs[3], eye))
    )
    mine = jnp.where(y == 0, pairs[0], jnp.where(y == 1, pairs[1], jnp.where(y == 2, pairs[2], pairs[3])))
    lone = jnp.concatenate(
        [
            lax.dynamic_slice_in_dim(odd, y * NX, NX, 0)[:, :WIDTH].reshape(S, S),
            lax.dynamic_slice_in_dim(odd, y * NX, 1, 0)[0, WIDTH:],
        ],
        axis=0,
    )
    group = after(jnp.where(core == 0, mine, lone), beyond)
    final = after(group, entry)
    factor_t = final[:WIDTH].astype(jnp.bfloat16)
    states = (final[WIDTH][None, :] + sub_offset[0]).astype(jnp.bfloat16)

    rows_t = obs_rows.T
    swapped = lax.ppermute(rows_t, "col", [(0, 1), (1, 0), (2, 3), (3, 2)])
    low = lax.rem(x, 2) == 0
    half = jnp.concatenate(
        [jnp.where(low, rows_t, swapped), jnp.where(low, swapped, rows_t)], axis=0
    )
    crossed_half = lax.ppermute(half, "col", [(0, 2), (2, 0), (1, 3), (3, 1)])
    low = x < 2
    all_rows = jnp.concatenate(
        [jnp.where(low, half, crossed_half), jnp.where(low, crossed_half, half)], axis=0
    )

    picks = jnp.dot(states, all_rows, preferred_element_type=jnp.float32)
    onehot = obs_step[None, :] == jnp.arange(SUB)[:, None]
    guess = jnp.sum(jnp.where(onehot, picks, jnp.float32(0.0)), axis=0)
    projected = jnp.dot(factor_t, all_rows, preferred_element_type=jnp.float32)
    spread = lax.psum(jnp.sum(projected * projected, axis=0), "col")
    live = (jnp.arange(rows_t.shape[1]) < obs_count[0]).astype(jnp.float32)
    return (guess * live, spread * live)


def solution(mesh):
    torus = Mesh(mesh.devices.reshape(NZ, NY, NC, NX), ("z", "y", "core", "col"))
    in_specs = (
        P(TM, None, "col"),
        P(TM, None),
        P(TM, None, None),
        P(),
        P(),
        P(TM, "col"),
        P(TM),
        P(TM),
    )
    out_specs = (P(TM), P(TM))
    return jax.shard_map(
        shards, mesh=torus, in_specs=in_specs, out_specs=out_specs, check_vma=False
    )
```

```python
import jax
import jax.numpy as jnp
from jax import lax
from jax.sharding import Mesh, PartitionSpec as P


S = 256
SUB = 8
NZ, NY, NC, NX = 16, 4, 2, 4
WIDTH = S // NX
CARRY = WIDTH + SUB
TM = ("z", "y", "core")
FINE = lax.Precision.HIGH


def tm_id(z, y, c):
    return (z * NY + y) * NC + c


def along_z(moves):
    return [(tm_id(a, y, 0), tm_id(b, y, 0)) for a, b in moves for y in range(NY)]


def tail_rows(vec):
    return jnp.zeros((SUB, S), jnp.float32).at[0].set(vec)


def after(outer, inner):
    rows = inner.shape[0] - SUB
    bias = jnp.concatenate([jnp.zeros((rows, S), jnp.float32), outer[S:]], axis=0)
    return jnp.dot(inner, outer[:S], precision=FINE) + bias


def packed(cols, state):
    row = lax.broadcasted_iota(jnp.int32, (CARRY, S), 0)
    high = lax.reduce_precision(state, 8, 7)
    low = state - high
    tail = jnp.where(row == WIDTH, high, jnp.where(row == WIDTH + 1, low, 0.0))
    return jnp.where(row < WIDTH, cols, tail).astype(jnp.bfloat16)


def moved(outer, carry):
    cols = jnp.dot(carry.astype(jnp.float32), outer[:S], precision=lax.Precision.HIGHEST)
    state = cols[WIDTH : WIDTH + 1] + cols[WIDTH + 1 : WIDTH + 2] + outer[S : S + 1]
    return cols, state


def hop(outer, carry):
    return packed(*moved(outer, carry))


def maps_of(raw, y):
    block = raw[y * NX : (y + 1) * NX, :WIDTH].reshape(S, S)
    return jnp.concatenate([block, raw[y * NX, WIDTH:]], axis=0)


def compute(
    gain, offset, sub_offset, terminal_state, terminal_factor, obs_rows, obs_count, obs_step
):
    core = lax.axis_index("core")
    z = lax.axis_index("z")
    y = lax.axis_index("y")
    x = lax.axis_index("col")
    place = lax.rem(z, 4)
    eye = jnp.eye(S + SUB, S, dtype=jnp.float32)

    own = jnp.concatenate([gain[0].T, tail_rows(offset[0])], axis=0)
    own = lax.all_to_all(
        jnp.broadcast_to(own, (NY * NX, WIDTH + SUB, S)), ("y", "col"), 0, 0
    )
    other = lax.ppermute(own, "core", [(0, 1), (1, 0)])
    even = jnp.where(core == 0, own, other)
    odd = jnp.where(core == 0, other, own)
    pairs = [after(maps_of(even, i), maps_of(odd, i)) for i in range(NY)]
    tail2 = after(pairs[2], pairs[3])
    tail3 = after(pairs[1], tail2)
    plane = after(pairs[0], tail3)

    top_cols = lax.dynamic_slice_in_dim(terminal_factor, x * WIDTH, WIDTH, 1).T
    top = packed(
        jnp.concatenate([top_cols, jnp.zeros((SUB, S), jnp.float32)], axis=0), terminal_state[None, :]
    )
    low_blocks = (0, 4, 8)

    near = lax.ppermute(
        plane, TM, along_z([(b + j + 1, b + j) for b in low_blocks for j in range(3)] + [(13, 12)])
    )
    head15 = hop(plane, top)
    at14 = lax.ppermute(head15, TM, along_z([(15, 14)]))
    head14 = hop(plane, at14)
    at12 = lax.ppermute(head14, TM, along_z([(14, 12)]))
    near = jnp.where(jnp.logical_or(place == 3, z >= 13), eye, near)
    two = after(plane, near)
    far0 = lax.ppermute(two, TM, along_z([(b + 2, b) for b in low_blocks]))
    head12 = hop(two, at12)
    at8 = lax.ppermute(head12, TM, along_z([(12, 8)]))
    whole = after(two, far0)
    head8 = hop(whole, at8)
    at4 = lax.ppermute(head8, TM, along_z([(8, 4)]))
    far1 = lax.ppermute(two, TM, along_z([(b + 3, b + 1) for b in low_blocks]))
    at13 = lax.ppermute(head14, TM, along_z([(14, 13)]))
    far = jnp.where(
        jnp.logical_and(place == 0, z < 12),
        far0,
        jnp.where(jnp.logical_and(place == 1, z < 12), far1, eye),
    )
    inside = after(near, far)
    head4 = hop(whole, at4)
    head = jnp.where(z == 12, head12, jnp.where(z == 8, head8, head4))
    at0 = lax.ppermute(head, TM, along_z([(4, 0)]))
    fans = []
    for j in (1, 2, 3):
        fans.append(lax.ppermute(head, TM, along_z([(b + 4, b + j) for b in low_blocks])))
    reached = jnp.where(z == 8, at8, jnp.where(z == 4, at4, at0))
    for j in (1, 2, 3):
        reached = jnp.where(place == j, fans[j - 1], reached)
    reached = jnp.where(z == 12, at12, jnp.where(z == 13, at13, jnp.where(z == 14, at14, reached)))
    reached = jnp.where(z == 15, top, reached)
    entry = hop(inside, reached)
    crossed = lax.ppermute(entry, "core", [(0, 1)])
    entry = jnp.where(core == 0, entry, crossed)

    beyond = jnp.where(
        y == 0, tail3, jnp.where(y == 1, tail2, jnp.where(y == 2, pairs[3], eye))
    )
    mine = jnp.where(y == 0, pairs[0], jnp.where(y == 1, pairs[1], jnp.where(y == 2, pairs[2], pairs[3])))
    lone = jnp.concatenate(
        [
            lax.dynamic_slice_in_dim(odd, y * NX, NX, 0)[:, :WIDTH].reshape(S, S),
            lax.dynamic_slice_in_dim(odd, y * NX, 1, 0)[0, WIDTH:],
        ],
        axis=0,
    )
    group = after(jnp.where(core == 0, mine, lone), beyond)
    cols, state = moved(group, entry)
    factor_t = cols[:WIDTH].astype(jnp.bfloat16)
    states = (state + sub_offset[0]).astype(jnp.bfloat16)

    rows_t = obs_rows.T
    swapped = lax.ppermute(rows_t, "col", [(0, 1), (1, 0), (2, 3), (3, 2)])
    low = lax.rem(x, 2) == 0
    half = jnp.concatenate(
        [jnp.where(low, rows_t, swapped), jnp.where(low, swapped, rows_t)], axis=0
    )
    crossed_half = lax.ppermute(half, "col", [(0, 2), (2, 0), (1, 3), (3, 1)])
    low = x < 2
    all_rows = jnp.concatenate(
        [jnp.where(low, half, crossed_half), jnp.where(low, crossed_half, half)], axis=0
    )

    picks = jnp.dot(states, all_rows, preferred_element_type=jnp.float32)
    onehot = obs_step[None, :] == jnp.arange(SUB)[:, None]
    guess = jnp.sum(jnp.where(onehot, picks, jnp.float32(0.0)), axis=0)
    projected = jnp.dot(factor_t, all_rows, preferred_element_type=jnp.float32)
    part = jnp.sum(projected * projected, axis=0)
    live = (jnp.arange(rows_t.shape[1]) < obs_count[0]).astype(jnp.float32)
    guess = guess * live
    part, guess = lax.optimization_barrier((part, guess))
    parts = lax.all_to_all(jnp.broadcast_to(part, (NX, part.shape[0])), "col", 0, 0)
    return (guess, jnp.sum(parts, axis=0) * live)


def solution(mesh):
    torus = Mesh(mesh.devices.reshape(NZ, NY, NC, NX), ("z", "y", "core", "col"))
    in_specs = (
        P(TM, None, "col"),
        P(TM, None),
        P(TM, None, None),
        P(),
        P(),
        P(TM, "col"),
        P(TM),
        P(TM),
    )
    out_specs = (P(TM), P(TM))
    return jax.shard_map(
        compute, mesh=torus, in_specs=in_specs, out_specs=out_specs, check_vma=False
    )
```

```python
import jax
import jax.numpy as jnp
from jax import lax
from jax.sharding import Mesh, PartitionSpec as P


S = 256
SUB = 8
NZ, NY, NC, NX = 16, 4, 2, 4
WIDTH = S // NX
CARRY = WIDTH + SUB
TM = ("z", "y", "core")
FINE = lax.Precision.HIGH


def tm_id(z, y, c):
    return (z * NY + y) * NC + c


def along_z(moves):
    return [(tm_id(a, y, 0), tm_id(b, y, 0)) for a, b in moves for y in range(NY)]


def tail_rows(vec):
    return jnp.zeros((SUB, S), jnp.float32).at[0].set(vec)


def after(outer, inner):
    rows = inner.shape[0] - SUB
    bias = jnp.concatenate([jnp.zeros((rows, S), jnp.float32), outer[S:]], axis=0)
    return jnp.dot(inner, outer[:S], precision=FINE) + bias


def packed(cols, state):
    row = lax.broadcasted_iota(jnp.int32, (CARRY, S), 0)
    high = lax.reduce_precision(state, 8, 7)
    low = state - high
    tail = jnp.where(row == WIDTH, high, jnp.where(row == WIDTH + 1, low, 0.0))
    return jnp.where(row < WIDTH, cols, tail).astype(jnp.bfloat16)


def moved(outer, carry):
    cols = jnp.dot(carry.astype(jnp.float32), outer[:S], precision=lax.Precision.HIGHEST)
    state = cols[WIDTH : WIDTH + 1] + cols[WIDTH + 1 : WIDTH + 2] + outer[S : S + 1]
    return cols, state


def hop(outer, carry):
    return packed(*moved(outer, carry))


def maps_of(raw, y):
    block = raw[y * NX : (y + 1) * NX, :WIDTH].reshape(S, S)
    return jnp.concatenate([block, raw[y * NX, WIDTH:]], axis=0)


def compute(
    gain, offset, sub_offset, terminal_state, terminal_factor, obs_rows, obs_count, obs_step
):
    core = lax.axis_index("core")
    z = lax.axis_index("z")
    y = lax.axis_index("y")
    x = lax.axis_index("col")
    place = lax.rem(z, 4)
    eye = jnp.eye(S + SUB, S, dtype=jnp.float32)

    own = jnp.concatenate([gain[0].T, tail_rows(offset[0])], axis=0)
    own = lax.all_to_all(
        jnp.broadcast_to(own, (NY * NX, WIDTH + SUB, S)), ("y", "col"), 0, 0
    )
    other = lax.ppermute(own, "core", [(0, 1), (1, 0)])
    even = jnp.where(core == 0, own, other)
    odd = jnp.where(core == 0, other, own)
    pairs = [after(maps_of(even, i), maps_of(odd, i)) for i in range(NY)]
    tail2 = after(pairs[2], pairs[3])
    tail3 = after(pairs[1], tail2)
    plane = after(pairs[0], tail3)

    top_cols = lax.dynamic_slice_in_dim(terminal_factor, x * WIDTH, WIDTH, 1).T
    top = packed(
        jnp.concatenate([top_cols, jnp.zeros((SUB, S), jnp.float32)], axis=0), terminal_state[None, :]
    )
    low_blocks = (0, 4, 8)

    near = lax.ppermute(
        plane, TM, along_z([(b + j + 1, b + j) for b in low_blocks for j in range(3)])
    )
    near12 = lax.ppermute(plane, TM, along_z([(13, 12)]))
    head15 = hop(plane, top)
    at14 = lax.ppermute(head15, TM, along_z([(15, 14)]))
    head14 = hop(plane, at14)
    at12 = lax.ppermute(head14, TM, along_z([(14, 12)]))
    two12 = after(plane, near12)
    head12 = hop(two12, at12)
    at8 = lax.ppermute(head12, TM, along_z([(12, 8)]))
    near = jnp.where(place == 3, eye, near)
    two = after(plane, near)
    far0 = lax.ppermute(two, TM, along_z([(b + 2, b) for b in low_blocks]))
    whole = after(two, far0)
    head8 = hop(whole, at8)
    at4 = lax.ppermute(head8, TM, along_z([(8, 4)]))
    far1 = lax.ppermute(two, TM, along_z([(b + 3, b + 1) for b in low_blocks]))
    at13 = lax.ppermute(head14, TM, along_z([(14, 13)]))
    far = jnp.where(
        jnp.logical_and(place == 0, z < 12),
        far0,
        jnp.where(jnp.logical_and(place == 1, z < 12), far1, eye),
    )
    inside = jnp.where(z > 12, eye, jnp.where(z == 12, near12, after(near, far)))
    head4 = hop(whole, at4)
    head = jnp.where(z == 12, head12, jnp.where(z == 8, head8, head4))
    at0 = lax.ppermute(head, TM, along_z([(4, 0)]))
    fans = []
    for j in (1, 2, 3):
        fans.append(lax.ppermute(head, TM, along_z([(b + 4, b + j) for b in low_blocks])))
    reached = jnp.where(z == 8, at8, jnp.where(z == 4, at4, at0))
    for j in (1, 2, 3):
        reached = jnp.where(place == j, fans[j - 1], reached)
    reached = jnp.where(z == 12, at12, jnp.where(z == 13, at13, jnp.where(z == 14, at14, reached)))
    reached = jnp.where(z == 15, top, reached)
    entry = hop(inside, reached)
    crossed = lax.ppermute(entry, "core", [(0, 1)])
    entry = jnp.where(core == 0, entry, crossed)

    beyond = jnp.where(
        y == 0, tail3, jnp.where(y == 1, tail2, jnp.where(y == 2, pairs[3], eye))
    )
    mine = jnp.where(y == 0, pairs[0], jnp.where(y == 1, pairs[1], jnp.where(y == 2, pairs[2], pairs[3])))
    lone = jnp.concatenate(
        [
            lax.dynamic_slice_in_dim(odd, y * NX, NX, 0)[:, :WIDTH].reshape(S, S),
            lax.dynamic_slice_in_dim(odd, y * NX, 1, 0)[0, WIDTH:],
        ],
        axis=0,
    )
    group = after(jnp.where(core == 0, mine, lone), beyond)
    cols, state = moved(group, entry)
    factor_t = cols[:WIDTH].astype(jnp.bfloat16)
    states = (state + sub_offset[0]).astype(jnp.bfloat16)

    rows_t = obs_rows.T
    swapped = lax.ppermute(rows_t, "col", [(0, 1), (1, 0), (2, 3), (3, 2)])
    low = lax.rem(x, 2) == 0
    half = jnp.concatenate(
        [jnp.where(low, rows_t, swapped), jnp.where(low, swapped, rows_t)], axis=0
    )
    crossed_half = lax.ppermute(half, "col", [(0, 2), (2, 0), (1, 3), (3, 1)])
    low = x < 2
    all_rows = jnp.concatenate(
        [jnp.where(low, half, crossed_half), jnp.where(low, crossed_half, half)], axis=0
    )

    picks = jnp.dot(states, all_rows, preferred_element_type=jnp.float32)
    onehot = obs_step[None, :] == jnp.arange(SUB)[:, None]
    guess = jnp.sum(jnp.where(onehot, picks, jnp.float32(0.0)), axis=0)
    projected = jnp.dot(factor_t, all_rows, preferred_element_type=jnp.float32)
    part = jnp.sum(projected * projected, axis=0)
    live = (jnp.arange(rows_t.shape[1]) < obs_count[0]).astype(jnp.float32)
    parts = lax.all_to_all(jnp.broadcast_to(part, (NX, part.shape[0])), "col", 0, 0)
    spread = (parts[0] + parts[1]) + (parts[2] + parts[3])
    return (guess * live, spread * live)


def solution(mesh):
    torus = Mesh(mesh.devices.reshape(NZ, NY, NC, NX), ("z", "y", "core", "col"))
    in_specs = (
        P(TM, None, "col"),
        P(TM, None),
        P(TM, None, None),
        P(),
        P(),
        P(TM, "col"),
        P(TM),
        P(TM),
    )
    out_specs = (P(TM), P(TM))
    return jax.shard_map(
        compute, mesh=torus, in_specs=in_specs, out_specs=out_specs, check_vma=False
    )
```

```python
import jax
import jax.numpy as jnp
from jax import lax
from jax.sharding import Mesh, PartitionSpec as P


S = 256
SUB = 8
NZ, NY, NC, NX = 16, 4, 2, 4
WIDTH = S // NX
COLS = S // 2
CARRY = COLS + SUB
TM = ("z", "y", "core")
FINE = lax.Precision.HIGH


def tm_id(z, y, c):
    return (z * NY + y) * NC + c


def along_z(moves):
    return [(tm_id(a, y, 0), tm_id(b, y, 0)) for a, b in moves for y in range(NY)]


def tail_rows(vec):
    return jnp.zeros((SUB, S), jnp.float32).at[0].set(vec)


def after(outer, inner):
    rows = inner.shape[0] - SUB
    bias = jnp.concatenate([jnp.zeros((rows, S), jnp.float32), outer[S:]], axis=0)
    return jnp.dot(inner, outer[:S], precision=FINE) + bias


def packed(cols, state):
    row = lax.broadcasted_iota(jnp.int32, (CARRY, S), 0)
    high = lax.reduce_precision(state, 8, 7)
    low = state - high
    tail = jnp.where(row == COLS, high, jnp.where(row == COLS + 1, low, 0.0))
    return jnp.where(row < COLS, cols, tail).astype(jnp.bfloat16)


def moved(outer, carry):
    cols = jnp.dot(carry.astype(jnp.float32), outer[:S], precision=FINE)
    state = cols[COLS : COLS + 1] + cols[COLS + 1 : COLS + 2] + outer[S : S + 1]
    return cols, state


def hop(outer, carry):
    return packed(*moved(outer, carry))


def maps_of(raw, y):
    block = raw[y * NX : (y + 1) * NX, :WIDTH].reshape(S, S)
    return jnp.concatenate([block, raw[y * NX, WIDTH:]], axis=0)


def compute(
    gain, offset, sub_offset, terminal_state, terminal_factor, obs_rows, obs_count, obs_step
):
    core = lax.axis_index("core")
    z = lax.axis_index("z")
    y = lax.axis_index("y")
    x = lax.axis_index("col")
    place = lax.rem(z, 4)
    eye = jnp.eye(S + SUB, S, dtype=jnp.float32)

    own = jnp.concatenate([gain[0].T, tail_rows(offset[0])], axis=0)
    own = lax.all_to_all(
        jnp.broadcast_to(own, (NY * NX, WIDTH + SUB, S)), ("y", "col"), 0, 0
    )
    other = lax.ppermute(own, "core", [(0, 1), (1, 0)])
    even = jnp.where(core == 0, own, other)
    odd = jnp.where(core == 0, other, own)
    pairs = [after(maps_of(even, i), maps_of(odd, i)) for i in range(NY)]
    tail2 = after(pairs[2], pairs[3])
    tail3 = after(pairs[1], tail2)
    plane = after(pairs[0], tail3)

    top_cols = lax.dynamic_slice_in_dim(terminal_factor, lax.rem(x, 2) * COLS, COLS, 1).T
    top = packed(
        jnp.concatenate([top_cols, jnp.zeros((SUB, S), jnp.float32)], axis=0), terminal_state[None, :]
    )
    low_blocks = (0, 4, 8)

    near = lax.ppermute(
        plane, TM, along_z([(b + j + 1, b + j) for b in low_blocks for j in range(3)])
    )
    near12 = lax.ppermute(plane, TM, along_z([(13, 12)]))
    head15 = hop(plane, top)
    at14 = lax.ppermute(head15, TM, along_z([(15, 14)]))
    head14 = hop(plane, at14)
    at12 = lax.ppermute(head14, TM, along_z([(14, 12)]))
    two12 = after(plane, near12)
    head12 = hop(two12, at12)
    at8 = lax.ppermute(head12, TM, along_z([(12, 8)]))
    near = jnp.where(place == 3, eye, near)
    two = after(plane, near)
    far0 = lax.ppermute(two, TM, along_z([(b + 2, b) for b in low_blocks]))
    whole = after(two, far0)
    head8 = hop(whole, at8)
    at4 = lax.ppermute(head8, TM, along_z([(8, 4)]))
    far1 = lax.ppermute(two, TM, along_z([(b + 3, b + 1) for b in low_blocks]))
    at13 = lax.ppermute(head14, TM, along_z([(14, 13)]))
    far = jnp.where(
        jnp.logical_and(place == 0, z < 12),
        far0,
        jnp.where(jnp.logical_and(place == 1, z < 12), far1, eye),
    )
    inside = jnp.where(z > 12, eye, jnp.where(z == 12, near12, after(near, far)))
    head4 = hop(whole, at4)
    head = jnp.where(z == 12, head12, jnp.where(z == 8, head8, head4))
    at0 = lax.ppermute(head, TM, along_z([(4, 0)]))
    fans = []
    for j in (1, 2, 3):
        fans.append(lax.ppermute(head, TM, along_z([(b + 4, b + j) for b in low_blocks])))
    reached = jnp.where(z == 8, at8, jnp.where(z == 4, at4, at0))
    for j in (1, 2, 3):
        reached = jnp.where(place == j, fans[j - 1], reached)
    reached = jnp.where(z == 12, at12, jnp.where(z == 13, at13, jnp.where(z == 14, at14, reached)))
    reached = jnp.where(z == 15, top, reached)
    entry = hop(inside, reached)
    crossed = lax.ppermute(entry, "core", [(0, 1)])
    entry = jnp.where(core == 0, entry, crossed)

    beyond = jnp.where(
        y == 0, tail3, jnp.where(y == 1, tail2, jnp.where(y == 2, pairs[3], eye))
    )
    mine = jnp.where(y == 0, pairs[0], jnp.where(y == 1, pairs[1], jnp.where(y == 2, pairs[2], pairs[3])))
    lone = jnp.concatenate(
        [
            lax.dynamic_slice_in_dim(odd, y * NX, NX, 0)[:, :WIDTH].reshape(S, S),
            lax.dynamic_slice_in_dim(odd, y * NX, 1, 0)[0, WIDTH:],
        ],
        axis=0,
    )
    group = after(jnp.where(core == 0, mine, lone), beyond)
    cols, state = moved(group, entry)
    factor_t = cols[:COLS].astype(jnp.bfloat16)
    states = (state + sub_offset[0]).astype(jnp.bfloat16)

    rows_t = obs_rows.T
    swapped = lax.ppermute(rows_t, "col", [(0, 1), (1, 0), (2, 3), (3, 2)])
    low = lax.rem(x, 2) == 0
    half = jnp.concatenate(
        [jnp.where(low, rows_t, swapped), jnp.where(low, swapped, rows_t)], axis=0
    )
    crossed_half = lax.ppermute(half, "col", [(0, 2), (2, 0), (1, 3), (3, 1)])
    low = x < 2
    all_rows = jnp.concatenate(
        [jnp.where(low, half, crossed_half), jnp.where(low, crossed_half, half)], axis=0
    )

    picks = jnp.dot(states, all_rows, preferred_element_type=jnp.float32)
    onehot = obs_step[None, :] == jnp.arange(SUB)[:, None]
    guess = jnp.sum(jnp.where(onehot, picks, jnp.float32(0.0)), axis=0)
    projected = jnp.dot(factor_t, all_rows, preferred_element_type=jnp.float32)
    part = jnp.sum(projected * projected, axis=0)
    live = (jnp.arange(rows_t.shape[1]) < obs_count[0]).astype(jnp.float32)
    spread = part + lax.ppermute(part, "col", [(0, 1), (1, 0), (2, 3), (3, 2)])
    return (guess * live, spread * live)


def solution(mesh):
    torus = Mesh(mesh.devices.reshape(NZ, NY, NC, NX), ("z", "y", "core", "col"))
    in_specs = (
        P(TM, None, "col"),
        P(TM, None),
        P(TM, None, None),
        P(),
        P(),
        P(TM, "col"),
        P(TM),
        P(TM),
    )
    out_specs = (P(TM), P(TM))
    return jax.shard_map(
        compute, mesh=torus, in_specs=in_specs, out_specs=out_specs, check_vma=False
    )
```

```python
import jax
import jax.numpy as jnp
from jax import lax
from jax.sharding import Mesh, PartitionSpec as P


S = 256
SUB = 8
NZ, NY, NC, NX = 16, 4, 2, 4
WIDTH = S // NX
COLS = S // 2
CARRY = COLS + SUB
TM = ("z", "y", "core")
FINE = lax.Precision.HIGH


def tm_id(z, y, c):
    return (z * NY + y) * NC + c


def along_z(moves):
    return [(tm_id(a, y, 0), tm_id(b, y, 0)) for a, b in moves for y in range(NY)]


def tail_rows(vec):
    return jnp.broadcast_to(vec[None, :], (SUB, S))


def after(outer, inner):
    rows = inner.shape[0] - SUB
    bias = jnp.concatenate([jnp.zeros((rows, S), jnp.float32), outer[S:]], axis=0)
    return jnp.dot(inner, outer[:S], precision=FINE) + bias


def packed(cols, state):
    row = lax.broadcasted_iota(jnp.int32, (CARRY, S), 0)
    high = lax.reduce_precision(state, 8, 7)
    low = state - high
    tail = jnp.where(row == COLS, high, jnp.where(row == COLS + 1, low, 0.0))
    return jnp.where(row < COLS, cols, tail).astype(jnp.bfloat16)


def moved(outer, carry):
    cols = jnp.dot(carry.astype(jnp.float32), outer[:S], precision=FINE)
    state = cols[COLS : COLS + 1] + cols[COLS + 1 : COLS + 2] + outer[S : S + 1]
    return cols, state


def hop(outer, carry):
    return packed(*moved(outer, carry))


def maps_of(raw):
    raw = raw.reshape(NY, NX, WIDTH + SUB, S)
    return raw[:, :, :WIDTH].reshape(NY, S, S), raw[:, 0, WIDTH:]


def compute(
    gain, offset, sub_offset, terminal_state, terminal_factor, obs_rows, obs_count, obs_step
):
    core = lax.axis_index("core")
    z = lax.axis_index("z")
    y = lax.axis_index("y")
    x = lax.axis_index("col")
    place = lax.rem(z, 4)
    eye = jnp.eye(S + SUB, S, dtype=jnp.float32)

    own = jnp.concatenate([gain[0].T, tail_rows(offset[0])], axis=0)
    own = lax.all_to_all(
        jnp.broadcast_to(own, (NY * NX, WIDTH + SUB, S)), ("y", "col"), 0, 0
    )
    other = lax.ppermute(own, "core", [(0, 1), (1, 0)])
    even = jnp.where(core == 0, own, other)
    odd = jnp.where(core == 0, other, own)
    (even_maps, even_tails), (odd_maps, odd_tails) = maps_of(even), maps_of(odd)
    bodies = jnp.einsum("bij,bjk->bik", odd_maps, even_maps, precision=FINE)
    tails = jnp.einsum("bij,bjk->bik", odd_tails, even_maps, precision=FINE) + even_tails
    pairs = [jnp.concatenate([bodies[i], tails[i]], axis=0) for i in range(NY)]
    tail2 = after(pairs[2], pairs[3])
    tail3 = after(pairs[1], tail2)
    plane = after(pairs[0], tail3)

    top_cols = lax.dynamic_slice_in_dim(terminal_factor, lax.rem(x, 2) * COLS, COLS, 1).T
    top = packed(
        jnp.concatenate([top_cols, jnp.zeros((SUB, S), jnp.float32)], axis=0), terminal_state[None, :]
    )
    low_blocks = (0, 4, 8)

    near = lax.ppermute(
        plane, TM, along_z([(b + j + 1, b + j) for b in low_blocks for j in range(3)])
    )
    near12 = lax.ppermute(plane, TM, along_z([(13, 12)]))
    head15 = hop(plane, top)
    at14 = lax.ppermute(head15, TM, along_z([(15, 14)]))
    head14 = hop(plane, at14)
    at12 = lax.ppermute(head14, TM, along_z([(14, 12)]))
    two12 = after(plane, near12)
    head12 = hop(two12, at12)
    at8 = lax.ppermute(head12, TM, along_z([(12, 8)]))
    near = jnp.where(place == 3, eye, near)
    two = after(plane, near)
    far0 = lax.ppermute(two, TM, along_z([(b + 2, b) for b in low_blocks]))
    whole = after(two, far0)
    head8 = hop(whole, at8)
    at4 = lax.ppermute(head8, TM, along_z([(8, 4)]))
    far1 = lax.ppermute(two, TM, along_z([(b + 3, b + 1) for b in low_blocks]))
    at13 = lax.ppermute(head14, TM, along_z([(14, 13)]))
    far = jnp.where(
        jnp.logical_and(place == 0, z < 12),
        far0,
        jnp.where(jnp.logical_and(place == 1, z < 12), far1, eye),
    )
    inside = jnp.where(z > 12, eye, jnp.where(z == 12, near12, after(near, far)))
    head4 = hop(whole, at4)
    head = jnp.where(z == 12, head12, jnp.where(z == 8, head8, head4))
    at0 = lax.ppermute(head, TM, along_z([(4, 0)]))
    fans = []
    for j in (1, 2, 3):
        fans.append(lax.ppermute(head, TM, along_z([(b + 4, b + j) for b in low_blocks])))
    reached = jnp.where(z == 8, at8, jnp.where(z == 4, at4, at0))
    for j in (1, 2, 3):
        reached = jnp.where(place == j, fans[j - 1], reached)
    reached = jnp.where(z == 12, at12, jnp.where(z == 13, at13, jnp.where(z == 14, at14, reached)))
    reached = jnp.where(z == 15, top, reached)
    entry = hop(inside, reached)
    crossed = lax.ppermute(entry, "core", [(0, 1)])
    entry = jnp.where(core == 0, entry, crossed)

    beyond = jnp.where(
        y == 0, tail3, jnp.where(y == 1, tail2, jnp.where(y == 2, pairs[3], eye))
    )
    mine = jnp.where(y == 0, pairs[0], jnp.where(y == 1, pairs[1], jnp.where(y == 2, pairs[2], pairs[3])))
    lone = jnp.concatenate(
        [
            lax.dynamic_slice_in_dim(odd, y * NX, NX, 0)[:, :WIDTH].reshape(S, S),
            lax.dynamic_slice_in_dim(odd, y * NX, 1, 0)[0, WIDTH:],
        ],
        axis=0,
    )
    group = after(jnp.where(core == 0, mine, lone), beyond)
    cols, state = moved(group, entry)
    factor_t = cols[:COLS].astype(jnp.bfloat16)
    states = (state + sub_offset[0]).astype(jnp.bfloat16)

    rows_t = obs_rows.T
    swapped = lax.ppermute(rows_t, "col", [(0, 1), (1, 0), (2, 3), (3, 2)])
    low = lax.rem(x, 2) == 0
    half = jnp.concatenate(
        [jnp.where(low, rows_t, swapped), jnp.where(low, swapped, rows_t)], axis=0
    )
    crossed_half = lax.ppermute(half, "col", [(0, 2), (2, 0), (1, 3), (3, 1)])
    low = x < 2
    all_rows = jnp.concatenate(
        [jnp.where(low, half, crossed_half), jnp.where(low, crossed_half, half)], axis=0
    )

    picks = jnp.dot(states, all_rows, preferred_element_type=jnp.float32)
    onehot = obs_step[None, :] == jnp.arange(SUB)[:, None]
    guess = jnp.sum(jnp.where(onehot, picks, jnp.float32(0.0)), axis=0)
    projected = jnp.dot(factor_t, all_rows, preferred_element_type=jnp.float32)
    part = jnp.sum(projected * projected, axis=0)
    live = (jnp.arange(rows_t.shape[1]) < obs_count[0]).astype(jnp.float32)
    spread = part + lax.ppermute(part, "col", [(0, 1), (1, 0), (2, 3), (3, 2)])
    return (guess * live, spread * live)


def solution(mesh):
    torus = Mesh(mesh.devices.reshape(NZ, NY, NC, NX), ("z", "y", "core", "col"))
    in_specs = (
        P(TM, None, "col"),
        P(TM, None),
        P(TM, None, None),
        P(),
        P(),
        P(TM, "col"),
        P(TM),
        P(TM),
    )
    out_specs = (P(TM), P(TM))
    return jax.shard_map(
        compute, mesh=torus, in_specs=in_specs, out_specs=out_specs, check_vma=False
    )
```
